32 devices in a mesh: cls: 4 (over x, core), prt: 8 (over z, y).
Axes of the slice: x: 2, y: 2, z: 4, core: 2. Of those that a mesh axis runs over, the one named last changes fastest.
Arguments:
- images: bfloat16 [4096, 7168], P(('cls', 'prt')), may hold values from -48 to 48
- projections: bfloat16 [8, 144, 7168], P('cls', None, 'prt'), may hold values from -5 to 5
- noise_weights: float32 [7168], replicated, may hold values from 0.005 to 0.03
- class_prior: float32 [8], replicated, may hold values from 0.05 to 1
- class_lists: int32 [4096, 2], P(('cls', 'prt')), may hold values from 0 to 7, all different within a row; in each aligned block of 128 rows (0 to 127, 128 to 255, ...) at most 40 rows name the same one
Outputs:
- class_sums: float32 [8, 144, 7168], P('cls', None, 'prt')
- class_weights: float32 [8, 144], P('cls')
- evidence: float32 [4096], P(('cls', 'prt'))
The draws below stay inside these ranges and needn't reach their ends.
Inputs may be any that keep to these rules, and one draw needn't show every extreme that they name: `class_lists`: each row names 2 different classes; in the rows of one device no class is named by more than 40 rows, a bound that some block reaches.
All inputs are finite; a program needn't handle non-finite values.
Results may differ from the reference program's by a relative error of at most 0.0066.
Values may be sent and summed in bfloat16 or wider, within the bound.
No kernel may reach another device: no remote copies, remote signals or barrier semaphores. Data moves between devices by JAX's collectives and lax.ppermute only.
A program may use at most 128 MiB of HBM per device.

```python
import math
import jax
import jax.numpy as jnp
import numpy as np
from jax import lax

K = 8
R = 144
C = 2
ROWS = 128
COEF2 = 7168
MOST = 40
NPART = 4096


def stack_of(key):
    return jnp.clip(jax.random.normal(jax.random.fold_in(key, 7), (K, R, COEF2), jnp.float32), -5.0, 5.0)


def draw_projections(key, part):
    return stack_of(key).astype(jnp.bfloat16)


def draw_images(key, part):
    values = jax.random.normal(jax.random.fold_in(key, 11), (NPART, COEF2), jnp.float32)
    return jnp.clip(values, -48.0, 48.0).astype(jnp.bfloat16)


def shared_out(rng, own, number, rows, amount, top, reach, skew):
    sequence = jax.random.permutation(rng, amount)
    heavy_load, ordinary = load_shares(amount, rows * top, reach, skew, True), load_shares(amount, rows * top, reach, skew, False)
    places = jnp.arange(amount)

    def named(tallies, rotation):
        used = int((tallies > 0).sum())
        fixed = max(1, used // 4)
        moved = fixed + (places - fixed + rotation * (used - fixed)) % max(1, amount - fixed)
        return jnp.zeros((amount,), jnp.int32).at[sequence[jnp.where(places < fixed, places, moved)]].set(jnp.asarray(tallies, jnp.int32))

    tallies = jnp.where(number % 4 == 0, named(heavy_load, number // 4), named(ordinary, number - number // 4 - 1))
    mixed = jax.random.permutation(jax.random.fold_in(own, 3), amount)
    source_of, sink = mixed[0:amount // 2 * 2:2], mixed[1:amount // 2 * 2:2]
    margin = jnp.minimum(tallies[source_of] - 1, reach - tallies[sink]) // 2
    margin = jnp.where((source_of == sequence[0]) | (sink == sequence[0]) | (tallies[sink] == 0), 0, jnp.maximum(margin, 0))
    moved = jax.random.randint(jax.random.fold_in(own, 4), (amount // 2,), 0, 1 << 20) % (margin + 1)
    tallies = tallies.at[source_of].add(-moved).at[sink].add(moved)
    items = jnp.searchsorted(jnp.cumsum(tallies), jnp.arange(rows * top), side="right").astype(jnp.int32)
    table = items.reshape(top, rows).T
    table = table[jax.random.permutation(jax.random.fold_in(own, 1), rows)]
    rotation = jax.random.randint(jax.random.fold_in(own, 2), (rows, 1), 0, top)
    return jnp.take_along_axis(table, (jnp.arange(top)[None, :] + rotation) % top, axis=1)


def load_shares(number_of, total, limit, slope, full):
    loads = [(1 << 20) // math.isqrt(rank ** slope) + 1 for rank in range(1, number_of + 1)]
    largest = limit if full else min(limit, max(-(-total // number_of), total * loads[0] // sum(loads)))
    least = 1 if total - largest >= number_of - 1 else 0
    holding, rest = [largest] + [least] * (number_of - 1), total - largest - least * (number_of - 1)
    while rest > 0:
        movable = [i for i in range(1, number_of) if holding[i] < largest] or [i for i in range(1, number_of) if holding[i] < limit]
        whole, remaining = sum([loads[i] for i in movable]), rest
        for i in movable:
            addition = min(limit - holding[i], max(1, remaining * loads[i] // whole), rest)
            holding[i] = holding[i] + addition
            rest = rest - addition
    return np.array(holding)


def setup_inputs(seed: int = 0) -> dict:
    splits = jax.random.split(jax.random.key(seed), 6)
    images = draw_images(jax.random.fold_in(splits[5], 71), 0)
    projections = draw_projections(jax.random.fold_in(splits[5], 71), 0)
    noise_weights = jnp.clip(jnp.exp(jax.random.uniform(splits[2], (COEF2,), jnp.float32, math.log(0.005), math.log(0.03))), 0.005, 0.03)
    class_prior = jnp.clip(jnp.exp(jax.random.uniform(splits[3], (K,), jnp.float32, math.log(0.05), math.log(1.0))), 0.05, 1.0)
    class_lists_keys = jax.random.split(jax.random.fold_in(splits[4], 1), NPART // ROWS)
    class_lists_turns = jax.random.permutation(jax.random.fold_in(splits[4], 3), NPART // ROWS)
    class_lists = jax.vmap(lambda own, number: shared_out(jax.random.fold_in(splits[4], 2), own, number, ROWS, K, C, MOST, 2))(class_lists_keys, class_lists_turns).reshape((NPART, C))
    return {"images": images, "projections": projections, "noise_weights": noise_weights, "class_prior": class_prior, "class_lists": class_lists}


def reference(images, projections, noise_weights, class_prior, class_lists):
    proj_float = projections.astype(jnp.float32)
    norms = 0.5 * jnp.sum(proj_float * proj_float * noise_weights[None, None, :], axis=2)
    weighted = (images.astype(jnp.float32) * noise_weights[None, :]).astype(jnp.bfloat16)
    flat = projections.reshape(K * R, COEF2)
    listed = jnp.any(class_lists[:, :, None] == jnp.arange(K, dtype=jnp.int32)[None, None, :], axis=1)
    log_prior = jnp.log(class_prior)
    blk = 1024 if NPART % 1024 == 0 else NPART
    count = NPART // blk

    def block(args):
        wrows, lrows = args
        cross = lax.dot_general(wrows, flat, (((1,), (1,)), ((), ())), preferred_element_type=jnp.float32).reshape(blk, K, R)
        score = cross - norms[None, :, :] + log_prior[None, :, None]
        score = jnp.where(lrows[:, :, None], score, -jnp.inf)
        top = jnp.max(score, axis=(1, 2))
        total = jnp.sum(jnp.exp(score - top[:, None, None]), axis=(1, 2))
        evid = top + jnp.log(total)
        post = jnp.exp(score - evid[:, None, None]).astype(jnp.bfloat16)
        return evid, post

    evid, post = lax.map(block, (weighted.reshape(count, blk, COEF2), listed.reshape(count, blk, K)))
    evidence = evid.reshape(NPART)
    post = post.reshape(NPART, K, R)
    sums = []
    for k in range(K):
        sums.append(jnp.dot(post[:, k, :].T, images, preferred_element_type=jnp.float32))
    class_sums = jnp.stack(sums, axis=0)
    class_weights = jnp.sum(post.astype(jnp.float32), axis=0)
    return class_sums, class_weights, evidence
```

```python
import functools

import jax
import jax.numpy as jnp
from jax import lax
from jax.experimental import pallas as pl
from jax.experimental.pallas import tpu as pltpu
from jax.sharding import PartitionSpec as P

MOST = 40
GROUP = 4
F32 = jnp.float32
BF16 = jnp.bfloat16
VMEM = pl.BlockSpec(memory_space=pltpu.VMEM)
SMEM = pl.BlockSpec(memory_space=pltpu.SMEM)


def dot(a, b, dims):
    return lax.dot_general(a, b, (dims, ((), ())), preferred_element_type=F32)


def call(body, out_shape, *args, smem=()):
    return pl.pallas_call(
        body,
        out_shape=out_shape,
        in_specs=[SMEM if i in smem else VMEM for i in range(len(args))],
        out_specs=jax.tree.map(lambda _: VMEM, out_shape),
    )(*args)


def targets(lists, first, count, blocks):
    rows = lists.shape[-1]
    upper = lax.broadcasted_iota(jnp.int32, (rows, rows), 0) <= lax.broadcasted_iota(
        jnp.int32, (rows, rows), 1
    )
    upper = upper.astype(F32).astype(BF16)
    out = []
    for k in range(count):
        named = [
            jnp.where((lists[e, 0:1] == first + k) | (lists[e, 1:2] == first + k), 1.0, 0.0)
            for e in range(blocks)
        ]
        pad = [jnp.zeros((8 - blocks, rows), F32)] if blocks < 8 else []
        stack = jnp.concatenate(named + pad, axis=0).astype(BF16)
        rank = dot(stack, upper, ((1,), (0,)))
        slots = [
            jnp.where(named[e] > 0, rank[e : e + 1] - 1.0 + e * MOST, -1.0) for e in range(blocks)
        ]
        out.append(slots)
    return out


def pick(slots, low, size):
    wide = jnp.broadcast_to(slots, (size, slots.shape[1]))
    row = lax.broadcasted_iota(jnp.int32, wide.shape, 0).astype(F32) + low
    return jnp.where(wide == row, 1.0, 0.0).astype(BF16)


def pack(pair):
    half = pair[0].shape[0] // 2
    tails = [t[a : a + half, 128:] for t in pair for a in (0, half)]
    return jnp.concatenate([t[:, :128] for t in pair] + [jnp.concatenate(tails, axis=1)], axis=0)


def unpack(wire, orient):
    half = orient // 2
    tail = wire[2 * orient :]
    out = []
    for k in range(2):
        rest = jnp.concatenate(
            [tail[:, (2 * k + a) * 32 : (2 * k + a + 1) * 32] for a in (0, 1)], axis=0
        )
        out.append(jnp.concatenate([wire[k * orient : (k + 1) * orient], rest], axis=1))
    return out


def norm_kernel(proj, weights, out):
    for k in range(proj.shape[0]):
        p = proj[k].astype(F32)
        out[k] = 0.5 * jnp.sum(p * p * weights[...], axis=1, keepdims=True)


def cross_kernel(first, *refs, blocks):
    images = refs[:blocks]
    lists, weights, proj, norms, compact, scores = refs[blocks:]
    count, orient, _ = proj.shape
    slots = targets(lists[...], first[0], count, blocks)
    parts = [[] for _ in range(count)]
    step = 2
    for e in range(0, blocks, step):
        rows = jnp.concatenate([images[i][...] for i in range(e, e + step)], axis=0)
        for k in range(count):
            sel = pick(jnp.concatenate(slots[k][e : e + step], axis=1), e * MOST, step * MOST)
            got = dot(sel, rows, ((1,), (0,)))
            compact[k, e * MOST : (e + step) * MOST, :] = got.astype(BF16)
            parts[k].append((got * weights[...]).astype(BF16))
    pair = []
    for k in range(count):
        weighted = jnp.concatenate(parts[k], axis=0)
        pair.append(dot(proj[k], weighted, ((1,), (1,))) - norms[k])
    scores[...] = pack(pair)


def split(x):
    a = x.astype(BF16)
    rest = x - a.astype(F32)
    b = rest.astype(BF16)
    return [a.astype(F32), b.astype(F32), (rest - b.astype(F32)).astype(BF16).astype(F32)]


def stats_kernel(first, prior, lists, *refs, blocks, parts):
    wires = refs[:parts]
    score, stats = refs[parts:]
    count, orient, width = score.shape
    total = wires[0][...]
    for w in wires[1:]:
        total = total + w[...]
    pair = unpack(total, orient)
    slots = targets(lists[...], first[0], count, blocks)
    for k in range(count):
        t = pair[k] + prior[first[0] + k]
        score[k] = t
        top = jnp.max(t, axis=0, keepdims=True)
        mass = jnp.sum(jnp.exp(t - top), axis=0, keepdims=True)
        rows = jnp.concatenate(split(top) + split(mass) + [jnp.zeros((2, width), F32)], axis=0)
        where = jnp.concatenate(slots[k], axis=1)
        got = dot(rows.astype(BF16), pick(where, 0, width), ((1,), (0,)))
        named = where >= 0
        stats[2 * k : 2 * k + 1] = jnp.where(named, got[0:1] + got[1:2] + got[2:3], -jnp.inf)
        stats[2 * k + 1 : 2 * k + 2] = jnp.where(named, got[3:4] + got[4:5] + got[5:6], 0.0)


def post_kernel(first, lists, score, *refs, blocks):
    stats = refs[:blocks]
    wire, evidence = refs[blocks:]
    count, orient, width = score.shape
    rows = lists.shape[-1]
    tops, masses = [], []
    for f in range(blocks):
        part = stats[f][...]
        part = jnp.concatenate([part[:, (e ^ f) * rows : ((e ^ f) + 1) * rows] for e in range(blocks)], axis=1)
        for k in range(count):
            tops.append(part[2 * k : 2 * k + 1])
            masses.append(part[2 * k + 1 : 2 * k + 2])
    top = functools.reduce(jnp.maximum, tops)
    mass = sum(m * jnp.exp(t - top) for t, m in zip(tops, masses))
    evid = top + jnp.log(mass)
    evidence[...] = evid[:, :rows]
    slots = targets(lists[...], first[0], count, blocks)
    lanes = blocks * rows
    left = jnp.concatenate(
        split(evid) + [jnp.ones((1, lanes), F32), jnp.zeros((4, lanes), F32)], axis=0
    ).astype(BF16)
    pair = []
    for k in range(count):
        sel = pick(jnp.concatenate(slots[k], axis=1), 0, width)
        got = dot(left, sel, ((1,), (1,)))
        at = got[0:1] + got[1:2] + got[2:3]
        used = got[3:4] > 0.5
        pair.append(jnp.where(used, jnp.exp(score[k] - at), 0.0).astype(BF16).astype(F32))
    wire[...] = pack(pair).astype(BF16)


def sums_kernel(*refs, parts, low, high, totals):
    wires, compact = refs[:parts], refs[parts : 2 * parts]
    out = refs[2 * parts]
    count, orient, _ = out.shape
    posts = [unpack(w[...].astype(F32), orient) for w in wires]
    for k in range(count):
        acc = None
        for d in range(parts):
            got = dot(posts[d][k].astype(BF16), compact[d][k, :, low:high], ((1,), (0,)))
            acc = got if acc is None else acc + got
        out[k] = acc.astype(out.dtype)
        if totals:
            refs[2 * parts + 1][k] = sum(jnp.sum(p[k], axis=1, keepdims=True) for p in posts)


def local(images, projections, noise_weights, class_prior, class_lists):
    classes = lax.axis_size("cls")
    ring = lax.axis_size("prt")
    group = GROUP
    high = ring // group
    rows = images.shape[0]
    count, orient, f = projections.shape
    c, p = lax.axis_index("cls"), lax.axis_index("prt")
    h0, g0 = p // group, p % group
    first = (c * count).astype(jnp.int32).reshape(1)
    wide = classes * MOST

    def swap(x, axis, bit):
        n = lax.axis_size(axis)
        return lax.ppermute(x, axis, [(i, i ^ bit) for i in range(n)])

    def columns(x, g):
        at = [((h0 ^ h) * group + g) * f for h in range(high)]
        return jnp.concatenate(
            [lax.dynamic_slice_in_dim(x, a, f, axis=x.ndim - 1) for a in at], axis=x.ndim - 1
        )

    lists0 = class_lists.T
    weights = columns(noise_weights[None, :], g0)
    mine = [columns(images, g0 ^ d) for d in range(group)]
    pieces = [mine[0]] + [swap(mine[d], "prt", d) for d in range(1, group)]
    lists = [lists0] + [swap(lists0, "prt", d) for d in range(1, group)]
    lists = jnp.stack(lists)[:, None]
    proj = jnp.concatenate(
        [projections] + [swap(projections, "prt", h * group) for h in range(1, high)], axis=2
    )
    norms = call(norm_kernel, jax.ShapeDtypeStruct((count, orient, 1), F32), proj, weights)

    blocks = [{0: x} for x in pieces]
    bit = classes // 2
    while bit:
        lists = jnp.concatenate([lists, swap(lists, "cls", bit)], axis=1)
        for d in range(group):
            blocks[d].update({e ^ bit: swap(x, "cls", bit) for e, x in list(blocks[d].items())})
        bit //= 2
    order = [0]
    bit = classes // 2
    while bit:
        order = order + [e ^ bit for e in order]
        bit //= 2
    place = [order.index(e) for e in range(classes)]
    lists = jnp.stack([lists[:, i] for i in place], axis=1)

    compact, wires = [], []
    for d in range(group):
        got = call(
            functools.partial(cross_kernel, blocks=classes),
            (
                jax.ShapeDtypeStruct((count, wide, high * f), BF16),
                jax.ShapeDtypeStruct((orient * 5 // 2, 128), F32),
            ),
            first,
            *[blocks[d][e] for e in range(classes)],
            lists[d],
            weights,
            proj,
            norms,
            smem=(0,),
        )
        compact.append(got[0])
        wires.append(got[1])

    scores = [wires[0]] + [swap(wires[d], "prt", d) for d in range(1, group)]
    score, stats = call(
        functools.partial(stats_kernel, blocks=classes, parts=group),
        (
            jax.ShapeDtypeStruct((count, orient, wide), F32),
            jax.ShapeDtypeStruct((2 * count, classes * rows), F32),
        ),
        first,
        jnp.log(class_prior),
        lists[0],
        *scores,
        smem=(0, 1),
    )
    shared = [stats] + [swap(stats, "cls", e) for e in range(1, classes)]
    post, evidence = call(
        functools.partial(post_kernel, blocks=classes),
        (
            jax.ShapeDtypeStruct((orient * 5 // 2, 128), BF16),
            jax.ShapeDtypeStruct((1, rows), F32),
        ),
        first,
        lists[0],
        score,
        *shared,
        smem=(0,),
    )
    posts = [post] + [swap(post, "prt", d) for d in range(1, group)]
    far = call(
        functools.partial(sums_kernel, parts=group, low=f, high=high * f, totals=False),
        jax.ShapeDtypeStruct((count, orient, (high - 1) * f), BF16),
        *posts,
        *compact,
    )
    came = [
        swap(far[:, :, (h - 1) * f : h * f], "prt", h * group) for h in range(1, high)
    ]
    near, totals = call(
        functools.partial(sums_kernel, parts=group, low=0, high=f, totals=True),
        (
            jax.ShapeDtypeStruct((count, orient, f), F32),
            jax.ShapeDtypeStruct((count, orient, 1), F32),
        ),
        *posts,
        *compact,
    )
    totals = totals.reshape(count, orient)
    class_sums = near
    for x in came:
        class_sums = class_sums + x.astype(F32)
    class_weights = totals
    for h in range(1, high):
        class_weights = class_weights + swap(totals, "prt", h * group)
    return class_sums, class_weights, evidence.reshape(rows)


def solution(mesh):
    return jax.shard_map(
        local,
        mesh=mesh,
        in_specs=(
            P(("cls", "prt"), None),
            P("cls", None, "prt"),
            P(),
            P(),
            P(("cls", "prt"), None),
        ),
        out_specs=(P("cls", None, "prt"), P("cls", None), P(("cls", "prt"))),
        check_vma=False,
    )
```
